32 devices in a mesh: groups: 1, rows: 2 (over y), chans: 8 (over z, x), cols: 2 (over core).
Axes of the slice: x: 2, y: 2, z: 4, core: 2. Of those that a mesh axis runs over, the one named last changes fastest.
Arguments:
- feature_map: bfloat16 [5, 512, 32, 256], P('groups', 'chans', 'rows', 'cols'), may hold values from -6 to 6
- taps_x: bfloat16 [512, 63], P('chans'), may hold values from -0.75 to 0.75
- taps_y: bfloat16 [512, 63], P('chans'), may hold values from -0.75 to 0.75
- mix_weight: bfloat16 [512, 512], replicated, may hold values from -0.25 to 0.25
- mix_bias: bfloat16 [512], replicated, may hold values from -3 to 3
Outputs:
- section_out: bfloat16 [5, 512, 32, 256], P('groups', 'chans', 'rows', 'cols')
The draws below stay inside these ranges and needn't reach their ends.
All inputs are finite; a program needn't handle non-finite values.
Results may differ from the reference program's by a relative error of at most 0.0048.
Values may be sent and summed in bfloat16 or wider, within the bound.
A program may use at most 64 MiB of HBM per device.

```python
import jax
import jax.numpy as jnp
from jax import lax

C = 512
KERNEL_TAPS = 63
COLUMN_DILATION = 2
ROW_DILATION = 2
TILES = 5
MAP_ROWS = 32
MAP_COLUMNS = 256


def level_of(key, extent, pieces, smallest, high):
    loudness, own = 1.0, jax.random.fold_in(key, 6)
    for position, shards_of in pieces:
        heights = jnp.exp(jax.random.uniform(jax.random.fold_in(own, position), (shards_of,), jnp.float32, smallest / len(pieces), high / len(pieces)))
        loudness = loudness * jnp.repeat(heights, extent[position] // shards_of).reshape([-1 if axis == position else 1 for axis in range(len(extent))])
    return loudness


def bell_draw(stream_key, extent, spread, most, cuts=(), kind=jnp.bfloat16):
    result = spread * jax.random.normal(stream_key, extent, jnp.float32)
    if cuts:
        result = result * level_of(stream_key, extent, cuts, -0.22, 0.18)
    return jnp.clip(result, -most, most).astype(kind)


def setup_inputs(seed: int = 0, part: int = 0) -> dict:
    key_of = jax.random.split(jax.random.key(seed), 6)
    part_splits = jax.random.split(jax.random.fold_in(key_of[5], part), 6)
    return {
        "feature_map": bell_draw(part_splits[0], (TILES, C, MAP_ROWS, MAP_COLUMNS), 1.0, 6.0, ((1, 8), (2, 2), (3, 2))),
        "taps_x": bell_draw(key_of[1], (C, KERNEL_TAPS), KERNEL_TAPS ** -0.5, 0.75, ((0, 8),)),
        "taps_y": bell_draw(key_of[2], (C, KERNEL_TAPS), KERNEL_TAPS ** -0.5, 0.75, ((0, 8),)),
        "mix_weight": bell_draw(key_of[3], (C, C), C ** -0.5, 0.25),
        "mix_bias": bell_draw(key_of[4], (C,), 0.5, 3.0),
    }


def kernel_sweep(border_padded, coefficients, dilation, axis, tally_count):
    array_shape = list(border_padded.shape)
    array_shape[axis] = tally_count
    total = jnp.zeros(tuple(array_shape), jnp.float32)
    for tap in range(coefficients.shape[-1]):
        window = lax.slice_in_dim(border_padded, tap * dilation, tap * dilation + tally_count, axis=axis)
        total = total + window.astype(jnp.float32) * coefficients[..., tap]
    return total


def reference(feature_map, taps_x, taps_y, mix_weight, mix_bias):
    column_extent = (KERNEL_TAPS // 2) * COLUMN_DILATION
    row_extent = (KERNEL_TAPS // 2) * ROW_DILATION
    column_coefficient = taps_x.astype(jnp.float32)[:, None, None, :]
    row_coefficient = taps_y.astype(jnp.float32)[:, None, None, :]
    weight_full = mix_weight.astype(jnp.float32)
    bias_full = mix_bias.astype(jnp.float32)[:, None, None]

    def one_tile(tile):
        border_padded = jnp.pad(tile, ((0, 0), (0, 0), (column_extent, column_extent)))
        column_direction = kernel_sweep(border_padded, column_coefficient, COLUMN_DILATION, 2, MAP_COLUMNS).astype(jnp.bfloat16)
        border_padded = jnp.pad(column_direction, ((0, 0), (row_extent, row_extent), (0, 0)))
        row_direction = kernel_sweep(border_padded, row_coefficient, ROW_DILATION, 1, MAP_ROWS).astype(jnp.bfloat16)
        mixed = jnp.einsum("oc,chw->ohw", weight_full, row_direction.astype(jnp.float32))
        branch = jax.nn.gelu(mixed + bias_full, approximate=True).astype(jnp.bfloat16)
        return (tile.astype(jnp.float32) + branch.astype(jnp.float32)).astype(jnp.bfloat16)

    return lax.map(one_tile, feature_map)
```

```python
import functools

import jax
import jax.numpy as jnp
from jax import lax
from jax.experimental import pallas as pl
from jax.experimental.pallas import tpu as pltpu
from jax.sharding import PartitionSpec as P

KERNEL_TAPS = 63
HALF = KERNEL_TAPS // 2
COLUMN_DILATION = 2
ROW_DILATION = 2
MESH = pl.DeviceIdType.MESH
BF16 = jnp.bfloat16
F32 = jnp.float32


def with_halo(block, sides, width):
    for axis, dim in sides:
        count = lax.axis_size(axis)
        forward = [(i, i + 1) for i in range(count - 1)]
        backward = [(target, source) for source, target in forward]
        low = lax.ppermute(
            lax.slice_in_dim(block, block.shape[dim] - width, None, axis=dim), axis, forward
        )
        high = lax.ppermute(lax.slice_in_dim(block, 0, width, axis=dim), axis, backward)
        block = jnp.concatenate([low, block, high], axis=dim)
    return block


def kernel_sweep(border_padded, coefficients, dilation, axis, tally_count):
    array_shape = list(border_padded.shape)
    array_shape[axis] = tally_count
    total = jnp.zeros(tuple(array_shape), jnp.float32)
    for tap in range(coefficients.shape[-1]):
        window = lax.slice_in_dim(
            border_padded, tap * dilation, tap * dilation + tally_count, axis=axis
        )
        total = total + window.astype(jnp.float32) * coefficients[..., tap]
    return total


def rows_pass(tall_rows, kernel):
    row_extent = KERNEL_TAPS // 2 * ROW_DILATION
    coefficients = kernel.astype(jnp.float32)[:, None, None, :]
    border_padded = jnp.pad(tall_rows, ((0, 0), (0, 0), (row_extent, row_extent), (0, 0)))
    return kernel_sweep(border_padded, coefficients, ROW_DILATION, 2, tall_rows.shape[2]).astype(
        jnp.bfloat16
    )


def x_pass(column_widened, taps_x, tally_count):
    column_coefficient = taps_x.astype(jnp.float32)[:, None, None, :]
    return kernel_sweep(column_widened, column_coefficient, COLUMN_DILATION, 3, tally_count).astype(
        jnp.bfloat16
    )


def per_device_general(feature_map, taps_x, taps_y, mix_weight, mix_bias):
    column_extent = KERNEL_TAPS // 2 * COLUMN_DILATION
    column_widened = with_halo(feature_map, (("cols", 3),), column_extent)
    column_direction = x_pass(column_widened, taps_x, feature_map.shape[3])
    tall_rows = lax.all_to_all(column_direction, "rows", split_axis=1, concat_axis=2, tiled=True)
    per_row = tall_rows.shape[1]
    offset = lax.axis_index("rows") * per_row
    kernel_part = lax.dynamic_slice_in_dim(taps_y, offset, per_row, 0)
    along_tall = rows_pass(tall_rows, kernel_part)
    row_direction = lax.all_to_all(along_tall, "rows", split_axis=2, concat_axis=1, tiled=True)
    spread = lax.all_to_all(row_direction, "chans", split_axis=2, concat_axis=1, tiled=True)
    mixed = jnp.einsum("oc,bchw->bohw", mix_weight, spread, preferred_element_type=jnp.float32)
    bias_full = mix_bias.astype(jnp.float32)[:, None, None]
    activated = jax.nn.gelu(mixed + bias_full, approximate=True).astype(jnp.bfloat16)
    branch = lax.all_to_all(activated, "chans", split_axis=1, concat_axis=2, tiled=True)
    return (feature_map.astype(jnp.float32) + branch.astype(jnp.float32)).astype(jnp.bfloat16)


def dot(a, b):
    return jnp.dot(a, b, preferred_element_type=F32)


def iota(shape, dim):
    return lax.broadcasted_iota(jnp.int32, shape, dim)


def section_kernel(
    dims,
    feat_hbm, tapx_ref, tapy_ref, weight_ref, bias_ref,
    out_ref,
    feat, whole, toep, rowmat, swap, biasb, xbuf, ybuf, gath, brch, back,
    loc_sem, asend, arecv, csend, crecv, dsend, drecv,
):
    T, nr, nch, nco, C, CB, H, W = dims
    quads = nr * nco
    cq = CB // quads
    FH, FW = nr * H, nco * W
    rp = H // nch
    r, ch, co = lax.axis_index("rows"), lax.axis_index("chans"), lax.axis_index("cols")
    q = r * nco + co

    def peer(dr, i, dc):
        return lax.rem(r + dr, nr), lax.rem(ch + i, nch), lax.rem(co + dc, nco)

    def dev(p):
        return {"rows": p[0], "chans": p[1], "cols": p[2]}

    barrier = pltpu.get_barrier_semaphore()

    def greet(i, skip_self):
        for dr in range(nr):
            for dc in range(nco):
                if skip_self and dr == 0 and dc == 0:
                    continue
                pl.semaphore_signal(
                    barrier, inc=1, device_id=dev(peer(dr, i, dc)), device_id_type=MESH
                )

    greet(0, True)

    @pl.loop(1, nch)
    def _(i):
        greet(i, False)

    own = pltpu.make_async_copy(feat_hbm, feat, loc_sem.at[0])
    own.start()
    mine = []
    for t in range(T):
        c = pltpu.make_async_copy(
            feat_hbm.at[t, pl.ds(pl.multiple_of(q * cq, cq), cq)],
            whole.at[t, :, pl.ds(pl.multiple_of(r * H, H), H), pl.ds(pl.multiple_of(co * W, W), W)],
            loc_sem.at[1 + t],
        )
        c.start()
        mine.append(c)

    pl.semaphore_wait(barrier, nr * nch * nco - 1)

    for t in range(T):
        for dr in range(nr):
            for dc in range(nco):
                if dr == 0 and dc == 0:
                    continue
                p = peer(dr, 0, dc)
                pq = p[0] * nco + p[2]
                pltpu.make_async_remote_copy(
                    src_ref=feat_hbm.at[t, pl.ds(pl.multiple_of(pq * cq, cq), cq)],
                    dst_ref=whole.at[
                        t, :, pl.ds(pl.multiple_of(r * H, H), H), pl.ds(pl.multiple_of(co * W, W), W)
                    ],
                    send_sem=asend,
                    recv_sem=arecv.at[t],
                    device_id=dev(p),
                    device_id_type=MESH,
                ).start()

    qs = pl.ds(pl.multiple_of(q * cq, cq), cq)
    tx = tapx_ref[qs, :]
    ty = tapy_ref[qs, :]
    tap = iota((KERNEL_TAPS, FW), 0)
    pos = iota((KERNEL_TAPS, FW), 1)
    d = lax.rem(HALF * COLUMN_DILATION - COLUMN_DILATION * tap + FW, FW)
    spread_x = dot(tx, (pos == d).astype(F32).astype(BF16))
    jj = iota((16, FW), 0)
    ww = iota((16, FW), 1)
    reach = HALF * COLUMN_DILATION
    for c in range(cq):
        base = jnp.broadcast_to(spread_x[c : c + 1, :], (16, FW))
        base = pltpu.roll(base, 0, 1, stride=1, stride_axis=0)
        for b in range(FW // 16):
            rolled = base if b == 0 else pltpu.roll(base, 16 * b, 1)
            delta = ww - jj - 16 * b
            keep = (delta <= reach) & (delta >= -reach)
            toep[c, pl.ds(16 * b, 16), :] = jnp.where(keep, rolled, 0.0).astype(BF16)

    KK = cq * FH
    tap = iota((KERNEL_TAPS, FH), 0)
    pos = iota((KERNEL_TAPS, FH), 1)
    own_channel = (iota((cq, KK), 1) // FH) == iota((cq, KK), 0)
    for h in range(FH):
        pick = (pos - h) == ROW_DILATION * (tap - HALF)
        one = dot(ty, pick.astype(F32).astype(BF16))
        tiled = jnp.concatenate([one] * cq, axis=1)
        rowmat[pl.ds(h * cq, cq), :] = jnp.where(own_channel, tiled, 0.0).astype(BF16)

    a = iota((16 * H, 16 * H), 0)
    b = iota((16 * H, 16 * H), 1)
    swap[...] = ((a // H == lax.rem(b, 16)) & (lax.rem(a, H) == b // 16)).astype(F32).astype(BF16)
    diag = jnp.where(
        iota((C, C), 0) == iota((C, C), 1), jnp.broadcast_to(bias_ref[...].astype(F32), (C, C)), 0.0
    )
    biasb[...] = dot(diag.astype(BF16), jnp.ones((C, W), BF16))

    for c in mine:
        c.wait()
    own.wait()

    block = ch * quads + q
    chan_rows = pl.ds(pl.multiple_of(block * cq, cq), cq)

    def conv(t):
        landed = whole.at[0, pl.ds(0, cq // quads * (quads - 1))]
        pltpu.make_async_copy(landed, landed, arecv.at[t]).wait()

        @pl.loop(0, cq)
        def _(c):
            xbuf[pl.ds(pl.multiple_of(c * FH, FH), FH), :] = dot(whole[t, c], toep[c]).astype(BF16)

        along = dot(rowmat[...], xbuf[...]).astype(BF16).reshape(FH, cq, FW)
        for k in range(nco):
            ybuf[t, k] = along[:, :, k * W : (k + 1) * W]

        def piece(p):
            return ybuf.at[t, p[2], pl.ds(p[0] * H + p[1] * rp, rp)]

        def push(i, dr, dc):
            p = peer(dr, i, dc)
            pltpu.make_async_remote_copy(
                src_ref=piece(p),
                dst_ref=gath.at[t, :, chan_rows, :],
                send_sem=csend,
                recv_sem=crecv.at[t],
                device_id=dev(p),
                device_id_type=MESH,
            ).start()

        @pl.loop(0, nch - 1)
        def _(s):
            i = lax.rem(s + nch // 2 - 1, nch - 1) + 1
            for dr in range(nr):
                for dc in range(nco):
                    push(i, dr, dc)

        for dr in range(nr):
            for dc in range(nco):
                if dr or dc:
                    push(0, dr, dc)
        pltpu.make_async_copy(
            piece((r, ch, co)), gath.at[t, :, chan_rows, :], crecv.at[t]
        ).start()

    def mix(t):
        pltpu.make_async_copy(gath.at[t], gath.at[t], crecv.at[t]).wait()
        for k in range(rp):
            v = dot(weight_ref[...], gath[t, k]) + biasb[...]
            inner = 0.7978845608028654 * (v + 0.044715 * (v * v * v))
            brch[t, k] = (0.5 * v * (1.0 + jnp.tanh(inner))).astype(BF16)

        def piece(pc):
            return brch.at[t, :, pl.ds(pl.multiple_of(pc * CB, CB), CB), :]

        spot = pl.ds(ch * rp, rp)

        @pl.loop(0, nch - 1)
        def _(s):
            i = lax.rem(s + nch // 2 - 1, nch - 1) + 1
            p = peer(0, i, 0)
            pltpu.make_async_remote_copy(
                src_ref=piece(p[1]),
                dst_ref=back.at[t, spot],
                send_sem=dsend,
                recv_sem=drecv.at[t],
                device_id=dev(p),
                device_id_type=MESH,
            ).start()

        pltpu.make_async_copy(piece(ch), back.at[t, spot], drecv.at[t]).start()

    def finish(t):
        pltpu.make_async_copy(back.at[t], back.at[t], drecv.at[t]).wait()
        for g in range(CB // 16):
            rows = back[t, :, g * 16 : (g + 1) * 16, :].reshape(H * 16, W)
            branch = dot(swap[...], rows).reshape(16, H, W)
            out_ref[t, g * 16 : (g + 1) * 16] = (
                feat[t, g * 16 : (g + 1) * 16].astype(F32) + branch
            ).astype(BF16)

    lag1, lag2 = 2, 4

    @pl.loop(0, T + lag2)
    def _(s):
        @pl.when(s < T)
        def _():
            conv(s)

        @pl.when((s >= lag1) & (s < T + lag1))
        def _():
            mix(s - lag1)

        @pl.when(s >= lag2)
        def _():
            finish(s - lag2)

    sent = whole.at[:, pl.ds(0, cq // quads * (quads - 1))]
    pltpu.make_async_copy(sent, sent, asend).wait()
    parts = nr * nch * nco
    sent = gath.at[:, :, pl.ds(0, C // parts * (parts - 1)), :]
    pltpu.make_async_copy(sent, sent, csend).wait()
    sent = brch.at[:, :, pl.ds(0, C // nch * (nch - 1)), :]
    pltpu.make_async_copy(sent, sent, dsend).wait()


def per_device(mesh, feature_map, taps_x, taps_y, mix_weight, mix_bias):
    T, CB, H, W = feature_map.shape
    C = mix_weight.shape[0]
    nr, nch, nco = (mesh.shape[a] for a in ("rows", "chans", "cols"))
    quads = nr * nco
    cq = CB // quads
    rp = H // max(nch, 1)
    FH, FW = nr * H, nco * W
    dims = (T, nr, nch, nco, C, CB, H, W)
    return pl.pallas_call(
        functools.partial(section_kernel, dims),
        out_shape=jax.ShapeDtypeStruct(feature_map.shape, BF16),
        in_specs=[pl.BlockSpec(memory_space=pl.ANY)]
        + [pl.BlockSpec(memory_space=pltpu.VMEM)] * 4,
        out_specs=pl.BlockSpec(memory_space=pltpu.VMEM),
        scratch_shapes=[
            pltpu.VMEM((T, CB, H, W), BF16),
            pltpu.VMEM((T, cq, FH, FW), BF16),
            pltpu.VMEM((cq, FW, FW), BF16),
            pltpu.VMEM((FH * cq, cq * FH), BF16),
            pltpu.VMEM((16 * H, 16 * H), BF16),
            pltpu.VMEM((C, W), F32),
            pltpu.VMEM((cq * FH, FW), BF16),
            pltpu.VMEM((T, nco, FH, cq, W), BF16),
            pltpu.VMEM((T, rp, C, W), BF16),
            pltpu.VMEM((T, rp, C, W), BF16),
            pltpu.VMEM((T, H, CB, W), BF16),
            pltpu.SemaphoreType.DMA((1 + T,)),
            pltpu.SemaphoreType.DMA,
            pltpu.SemaphoreType.DMA((T,)),
            pltpu.SemaphoreType.DMA,
            pltpu.SemaphoreType.DMA((T,)),
            pltpu.SemaphoreType.DMA,
            pltpu.SemaphoreType.DMA((T,)),
        ],
        compiler_params=pltpu.CompilerParams(
            collective_id=0, has_side_effects=True, vmem_limit_bytes=40 * 1024 * 1024
        ),
    )(feature_map, taps_x, taps_y, mix_weight, mix_bias.reshape(1, C))


def fits_kernel(mesh):
    return mesh.shape["rows"] == 2 and mesh.shape["cols"] == 2 and mesh.shape["chans"] == 8


def solution(mesh):
    body = functools.partial(per_device, mesh) if fits_kernel(mesh) else per_device_general
    return jax.shard_map(
        body,
        mesh=mesh,
        in_specs=(
            P("groups", "chans", "rows", "cols"),
            P("chans", None),
            P("chans", None),
            P(),
            P(),
        ),
        out_specs=P("groups", "chans", "rows", "cols"),
        check_vma=False,
    )
```

```python
import functools

import jax
import jax.numpy as jnp
from jax import lax
from jax.experimental import pallas as pl
from jax.experimental.pallas import tpu as pltpu
from jax.sharding import PartitionSpec as P

KERNEL_TAPS = 63
HALF = KERNEL_TAPS // 2
COLUMN_DILATION = 2
ROW_DILATION = 2
MESH = pl.DeviceIdType.MESH
BF16 = jnp.bfloat16
F32 = jnp.float32


def with_halo(block, sides, width):
    for axis, dim in sides:
        count = lax.axis_size(axis)
        forward = [(i, i + 1) for i in range(count - 1)]
        backward = [(target, source) for source, target in forward]
        low = lax.ppermute(
            lax.slice_in_dim(block, block.shape[dim] - width, None, axis=dim), axis, forward
        )
        high = lax.ppermute(lax.slice_in_dim(block, 0, width, axis=dim), axis, backward)
        block = jnp.concatenate([low, block, high], axis=dim)
    return block


def kernel_sweep(border_padded, coefficients, dilation, axis, tally_count):
    array_shape = list(border_padded.shape)
    array_shape[axis] = tally_count
    total = jnp.zeros(tuple(array_shape), jnp.float32)
    for tap in range(coefficients.shape[-1]):
        window = lax.slice_in_dim(
            border_padded, tap * dilation, tap * dilation + tally_count, axis=axis
        )
        total = total + window.astype(jnp.float32) * coefficients[..., tap]
    return total


def rows_pass(tall_rows, kernel):
    row_extent = KERNEL_TAPS // 2 * ROW_DILATION
    coefficients = kernel.astype(jnp.float32)[:, None, None, :]
    border_padded = jnp.pad(tall_rows, ((0, 0), (0, 0), (row_extent, row_extent), (0, 0)))
    return kernel_sweep(border_padded, coefficients, ROW_DILATION, 2, tall_rows.shape[2]).astype(
        jnp.bfloat16
    )


def x_pass(column_widened, taps_x, tally_count):
    column_coefficient = taps_x.astype(jnp.float32)[:, None, None, :]
    return kernel_sweep(column_widened, column_coefficient, COLUMN_DILATION, 3, tally_count).astype(
        jnp.bfloat16
    )


def per_device_general(feature_map, taps_x, taps_y, mix_weight, mix_bias):
    column_extent = KERNEL_TAPS // 2 * COLUMN_DILATION
    column_widened = with_halo(feature_map, (("cols", 3),), column_extent)
    column_direction = x_pass(column_widened, taps_x, feature_map.shape[3])
    tall_rows = lax.all_to_all(column_direction, "rows", split_axis=1, concat_axis=2, tiled=True)
    per_row = tall_rows.shape[1]
    offset = lax.axis_index("rows") * per_row
    kernel_part = lax.dynamic_slice_in_dim(taps_y, offset, per_row, 0)
    along_tall = rows_pass(tall_rows, kernel_part)
    row_direction = lax.all_to_all(along_tall, "rows", split_axis=2, concat_axis=1, tiled=True)
    spread = lax.all_to_all(row_direction, "chans", split_axis=2, concat_axis=1, tiled=True)
    mixed = jnp.einsum("oc,bchw->bohw", mix_weight, spread, preferred_element_type=jnp.float32)
    bias_full = mix_bias.astype(jnp.float32)[:, None, None]
    activated = jax.nn.gelu(mixed + bias_full, approximate=True).astype(jnp.bfloat16)
    branch = lax.all_to_all(activated, "chans", split_axis=1, concat_axis=2, tiled=True)
    return (feature_map.astype(jnp.float32) + branch.astype(jnp.float32)).astype(jnp.bfloat16)


def dot(a, b):
    return jnp.dot(a, b, preferred_element_type=F32)


def iota(shape, dim):
    return lax.broadcasted_iota(jnp.int32, shape, dim)


def section_kernel(
    dims,
    feat_hbm, tapx_hbm, tapy_hbm, weight_hbm, bias_hbm,
    out_ref,
    tapx_ref, tapy_ref, weight_ref, bias_ref,
    feat, whole, toep, rowmat, swap, biasb, xbuf, ybuf, gath, brch, back,
    loc_sem, asend, arecv, csend, crecv, dsend, drecv,
):
    T, nr, nch, nco, C, CB, H, W = dims
    quads = nr * nco
    cq = CB // quads
    FH, FW = nr * H, nco * W
    rp = H // nch
    r, ch, co = lax.axis_index("rows"), lax.axis_index("chans"), lax.axis_index("cols")
    q = r * nco + co

    def peer(dr, i, dc):
        return lax.rem(r + dr, nr), lax.rem(ch + i, nch), lax.rem(co + dc, nco)

    def dev(p):
        return {"rows": p[0], "chans": p[1], "cols": p[2]}

    barrier = pltpu.get_barrier_semaphore()

    def greet(i, skip_self):
        for dr in range(nr):
            for dc in range(nco):
                if skip_self and dr == 0 and dc == 0:
                    continue
                pl.semaphore_signal(
                    barrier, inc=1, device_id=dev(peer(dr, i, dc)), device_id_type=MESH
                )

    greet(0, True)

    @pl.loop(1, nch)
    def _(i):
        greet(i, False)

    small = []
    for k, (src, dst) in enumerate(
        ((tapx_hbm, tapx_ref), (tapy_hbm, tapy_ref), (bias_hbm, bias_ref), (weight_hbm, weight_ref))
    ):
        c = pltpu.make_async_copy(src, dst, loc_sem.at[1 + T + k])
        c.start()
        small.append(c)
    own = pltpu.make_async_copy(feat_hbm, feat, loc_sem.at[0])
    mine = []
    for t in range(T):
        c = pltpu.make_async_copy(
            feat_hbm.at[t, pl.ds(pl.multiple_of(q * cq, cq), cq)],
            whole.at[t, r, co],
            loc_sem.at[1 + t],
        )
        c.start()
        mine.append(c)

    pl.semaphore_wait(barrier, nr * nch * nco - 1)

    cs = cq // nch

    def share(t, first, count):
        for dr in range(nr - 1, -1, -1):
            for dc in range(nco):
                if dr == 0 and dc == 0:
                    continue
                p = peer(dr, 0, dc)
                pq = p[0] * nco + p[2]
                pltpu.make_async_remote_copy(
                    src_ref=feat_hbm.at[t, pl.ds(pq * cq + first, count)],
                    dst_ref=whole.at[t, r, co, pl.ds(first, count)],
                    send_sem=asend,
                    recv_sem=arecv.at[t],
                    device_id=dev(p),
                    device_id_type=MESH,
                ).start()

    ahead = 2
    for t in range(min(ahead, T)):
        share(t, 0, cq)

    own.start()

    for c in small:
        c.wait()
    qs = pl.ds(pl.multiple_of(q * cq, cq), cq)
    tx = tapx_ref[qs, :]
    ty = tapy_ref[qs, :]
    tap = iota((KERNEL_TAPS, FW), 0)
    pos = iota((KERNEL_TAPS, FW), 1)
    d = lax.rem(HALF * COLUMN_DILATION - COLUMN_DILATION * tap + FW, FW)
    spread_x = dot(tx, (pos == d).astype(F32).astype(BF16))
    jj = iota((16, FW), 0)
    ww = iota((16, FW), 1)
    reach = HALF * COLUMN_DILATION
    for c in range(cq):
        base = jnp.broadcast_to(spread_x[c : c + 1, :], (16, FW))
        base = pltpu.roll(base, 0, 1, stride=1, stride_axis=0)
        for b in range(FW // 16):
            rolled = base if b == 0 else pltpu.roll(base, 16 * b, 1)
            delta = ww - jj - 16 * b
            keep = (delta <= reach) & (delta >= -reach)
            toep[c, pl.ds(16 * b, 16), :] = jnp.where(keep, rolled, 0.0).astype(BF16)

    KK = cq * FH
    tap = iota((KERNEL_TAPS, FH), 0)
    pos = iota((KERNEL_TAPS, FH), 1)
    own_channel = (iota((cq, KK), 1) // FH) == iota((cq, KK), 0)
    for h in range(FH):
        pick = (pos - h) == ROW_DILATION * (tap - HALF)
        one = dot(ty, pick.astype(F32).astype(BF16))
        tiled = jnp.concatenate([one] * cq, axis=1)
        rowmat[pl.ds(h * cq, cq), :] = jnp.where(own_channel, tiled, 0.0).astype(BF16)

    a = iota((16 * H, 16 * H), 0)
    b = iota((16 * H, 16 * H), 1)
    swap[...] = ((a // H == lax.rem(b, 16)) & (lax.rem(a, H) == b // 16)).astype(F32).astype(BF16)
    diag = jnp.where(
        iota((C, C), 0) == iota((C, C), 1), jnp.broadcast_to(bias_ref[...].astype(F32).reshape(1, C), (C, C)), 0.0
    )
    biasb[...] = dot(diag.astype(BF16), jnp.ones((C, W), BF16))

    for c in mine:
        c.wait()
    own.wait()

    block = ch * quads + q
    chan_rows = pl.ds(pl.multiple_of(block * cq, cq), cq)

    def full_map(t, c):
        bands = [
            jnp.concatenate([whole[t, i, j, c] for j in range(nco)], axis=1) for i in range(nr)
        ]
        return jnp.concatenate(bands, axis=0)

    def conv(t):
        landed = whole.at[0, :, :, pl.ds(0, cq // quads * (quads - 1))]
        pltpu.make_async_copy(landed, landed, arecv.at[t]).wait()

        @pl.loop(0, cq, unroll=4)
        def _(c):
            xbuf[pl.ds(pl.multiple_of(c * FH, FH), FH), :] = dot(full_map(t, c), toep[c]).astype(BF16)

        along = dot(rowmat[...], xbuf[...]).astype(BF16).reshape(FH, cq, FW)
        for k in range(nco):
            ybuf[t, k] = along[:, :, k * W : (k + 1) * W]

        def piece(p):
            return ybuf.at[t, p[2], pl.ds(p[0] * H + p[1] * rp, rp)]

        def push(i, dr, dc):
            p = peer(dr, i, dc)
            pltpu.make_async_remote_copy(
                src_ref=piece(p),
                dst_ref=gath.at[t, :, chan_rows, :],
                send_sem=csend,
                recv_sem=crecv.at[t],
                device_id=dev(p),
                device_id_type=MESH,
            ).start()

        @pl.loop(0, nch - 1)
        def _(s):
            @pl.when(t + ahead < T)
            def _():
                share(t + ahead, s * cs, cs)

            i = s + 1
            for dr in range(nr):
                for dc in range(nco):
                    push(i, dr, dc)

        @pl.when(t + ahead < T)
        def _():
            share(t + ahead, (nch - 1) * cs, cs)

        for dr in range(nr):
            for dc in range(nco):
                if dr or dc:
                    push(0, dr, dc)
        pltpu.make_async_copy(
            piece((r, ch, co)), gath.at[t, :, chan_rows, :], crecv.at[t]
        ).start()

    def mix(t):
        pltpu.make_async_copy(gath.at[t], gath.at[t], crecv.at[t]).wait()
        for k in range(rp):
            v = dot(weight_ref[...], gath[t, k]) + biasb[...]
            inner = 0.7978845608028654 * (v + 0.044715 * (v * v * v))
            brch[t, k] = (0.5 * v * (1.0 + jnp.tanh(inner))).astype(BF16)

        def piece(pc):
            return brch.at[t, :, pl.ds(pl.multiple_of(pc * CB, CB), CB), :]

        spot = pl.ds(ch * rp, rp)

        @pl.loop(0, nch - 1)
        def _(s):
            i = s + 1
            p = peer(0, i, 0)
            pltpu.make_async_remote_copy(
                src_ref=piece(p[1]),
                dst_ref=back.at[t, spot],
                send_sem=dsend,
                recv_sem=drecv.at[t],
                device_id=dev(p),
                device_id_type=MESH,
            ).start()

        pltpu.make_async_copy(piece(ch), back.at[t, spot], drecv.at[t]).start()

    def finish(t):
        pltpu.make_async_copy(back.at[t], back.at[t], drecv.at[t]).wait()
        for g in range(CB // 16):
            rows = back[t, :, g * 16 : (g + 1) * 16, :].reshape(H * 16, W)
            branch = dot(swap[...], rows).reshape(16, H, W)
            out_ref[t, g * 16 : (g + 1) * 16] = (
                feat[t, g * 16 : (g + 1) * 16].astype(F32) + branch
            ).astype(BF16)

    lag1, lag2 = 2, 4

    @pl.loop(0, T + lag2)
    def _(s):
        @pl.when(s < T)
        def _():
            conv(s)

        @pl.when((s >= lag1) & (s < T + lag1))
        def _():
            mix(s - lag1)

        @pl.when(s >= lag2)
        def _():
            finish(s - lag2)

    sent = whole.at[:, :, :, pl.ds(0, cq // quads * (quads - 1))]
    pltpu.make_async_copy(sent, sent, asend).wait()
    parts = nr * nch * nco
    sent = gath.at[:, :, pl.ds(0, C // parts * (parts - 1)), :]
    pltpu.make_async_copy(sent, sent, csend).wait()
    sent = brch.at[:, :, pl.ds(0, C // nch * (nch - 1)), :]
    pltpu.make_async_copy(sent, sent, dsend).wait()


def per_device(mesh, feature_map, taps_x, taps_y, mix_weight, mix_bias):
    T, CB, H, W = feature_map.shape
    C = mix_weight.shape[0]
    nr, nch, nco = (mesh.shape[a] for a in ("rows", "chans", "cols"))
    quads = nr * nco
    cq = CB // quads
    rp = H // max(nch, 1)
    FH, FW = nr * H, nco * W
    dims = (T, nr, nch, nco, C, CB, H, W)
    return pl.pallas_call(
        functools.partial(section_kernel, dims),
        out_shape=jax.ShapeDtypeStruct(feature_map.shape, BF16),
        in_specs=[pl.BlockSpec(memory_space=pltpu.HBM)] * 5,
        out_specs=pl.BlockSpec(memory_space=pltpu.VMEM),
        scratch_shapes=[
            pltpu.VMEM(taps_x.shape, BF16),
            pltpu.VMEM(taps_y.shape, BF16),
            pltpu.VMEM(mix_weight.shape, BF16),
            pltpu.VMEM((C,), BF16),
            pltpu.VMEM((T, CB, H, W), BF16),
            pltpu.VMEM((T, nr, nco, cq, H, W), BF16),
            pltpu.VMEM((cq, FW, FW), BF16),
            pltpu.VMEM((FH * cq, cq * FH), BF16),
            pltpu.VMEM((16 * H, 16 * H), BF16),
            pltpu.VMEM((C, W), F32),
            pltpu.VMEM((cq * FH, FW), BF16),
            pltpu.VMEM((T, nco, FH, cq, W), BF16),
            pltpu.VMEM((T, rp, C, W), BF16),
            pltpu.VMEM((T, rp, C, W), BF16),
            pltpu.VMEM((T, H, CB, W), BF16),
            pltpu.SemaphoreType.DMA((5 + T,)),
            pltpu.SemaphoreType.DMA,
            pltpu.SemaphoreType.DMA((T,)),
            pltpu.SemaphoreType.DMA,
            pltpu.SemaphoreType.DMA((T,)),
            pltpu.SemaphoreType.DMA,
            pltpu.SemaphoreType.DMA((T,)),
        ],
        compiler_params=pltpu.CompilerParams(
            collective_id=0, has_side_effects=True, vmem_limit_bytes=40 * 1024 * 1024
        ),
    )(*(pltpu.with_memory_space_constraint(v, pltpu.HBM) for v in (feature_map, taps_x, taps_y, mix_weight, mix_bias)))


def fits_kernel(mesh):
    return mesh.shape["rows"] == 2 and mesh.shape["cols"] == 2 and mesh.shape["chans"] == 8


def solution(mesh):
    body = functools.partial(per_device, mesh) if fits_kernel(mesh) else per_device_general
    return jax.shard_map(
        body,
        mesh=mesh,
        in_specs=(
            P("groups", "chans", "rows", "cols"),
            P("chans", None),
            P("chans", None),
            P(),
            P(),
        ),
        out_specs=P("groups", "chans", "rows", "cols"),
        check_vma=False,
    )
```

```python
import functools

import jax
import jax.numpy as jnp
from jax import lax
from jax.experimental import pallas as pl
from jax.experimental.pallas import tpu as pltpu
from jax.sharding import PartitionSpec as P

KERNEL_TAPS = 63
HALF = KERNEL_TAPS // 2
COLUMN_DILATION = 2
ROW_DILATION = 2
MESH = pl.DeviceIdType.MESH
BF16 = jnp.bfloat16
F32 = jnp.float32


def with_halo(block, sides, width):
    for axis, dim in sides:
        count = lax.axis_size(axis)
        forward = [(i, i + 1) for i in range(count - 1)]
        backward = [(target, source) for source, target in forward]
        low = lax.ppermute(
            lax.slice_in_dim(block, block.shape[dim] - width, None, axis=dim), axis, forward
        )
        high = lax.ppermute(lax.slice_in_dim(block, 0, width, axis=dim), axis, backward)
        block = jnp.concatenate([low, block, high], axis=dim)
    return block


def kernel_sweep(border_padded, coefficients, dilation, axis, tally_count):
    array_shape = list(border_padded.shape)
    array_shape[axis] = tally_count
    total = jnp.zeros(tuple(array_shape), jnp.float32)
    for tap in range(coefficients.shape[-1]):
        window = lax.slice_in_dim(
            border_padded, tap * dilation, tap * dilation + tally_count, axis=axis
        )
        total = total + window.astype(jnp.float32) * coefficients[..., tap]
    return total


def rows_pass(tall_rows, kernel):
    row_extent = KERNEL_TAPS // 2 * ROW_DILATION
    coefficients = kernel.astype(jnp.float32)[:, None, None, :]
    border_padded = jnp.pad(tall_rows, ((0, 0), (0, 0), (row_extent, row_extent), (0, 0)))
    return kernel_sweep(border_padded, coefficients, ROW_DILATION, 2, tall_rows.shape[2]).astype(
        jnp.bfloat16
    )


def x_pass(column_widened, taps_x, tally_count):
    column_coefficient = taps_x.astype(jnp.float32)[:, None, None, :]
    return kernel_sweep(column_widened, column_coefficient, COLUMN_DILATION, 3, tally_count).astype(
        jnp.bfloat16
    )


def per_device_general(feature_map, taps_x, taps_y, mix_weight, mix_bias):
    column_extent = KERNEL_TAPS // 2 * COLUMN_DILATION
    column_widened = with_halo(feature_map, (("cols", 3),), column_extent)
    column_direction = x_pass(column_widened, taps_x, feature_map.shape[3])
    tall_rows = lax.all_to_all(column_direction, "rows", split_axis=1, concat_axis=2, tiled=True)
    per_row = tall_rows.shape[1]
    offset = lax.axis_index("rows") * per_row
    kernel_part = lax.dynamic_slice_in_dim(taps_y, offset, per_row, 0)
    along_tall = rows_pass(tall_rows, kernel_part)
    row_direction = lax.all_to_all(along_tall, "rows", split_axis=2, concat_axis=1, tiled=True)
    spread = lax.all_to_all(row_direction, "chans", split_axis=2, concat_axis=1, tiled=True)
    mixed = jnp.einsum("oc,bchw->bohw", mix_weight, spread, preferred_element_type=jnp.float32)
    bias_full = mix_bias.astype(jnp.float32)[:, None, None]
    activated = jax.nn.gelu(mixed + bias_full, approximate=True).astype(jnp.bfloat16)
    branch = lax.all_to_all(activated, "chans", split_axis=1, concat_axis=2, tiled=True)
    return (feature_map.astype(jnp.float32) + branch.astype(jnp.float32)).astype(jnp.bfloat16)


def dot(a, b):
    return jnp.dot(a, b, preferred_element_type=F32)


def iota(shape, dim):
    return lax.broadcasted_iota(jnp.int32, shape, dim)


def section_kernel(
    dims,
    feat_hbm, tapx_hbm, tapy_hbm, weight_hbm, bias_hbm,
    out_ref,
    tapx_ref, tapy_ref, weight_ref, bias_ref,
    feat, whole, toep, rowmat, swap, biasb, xbuf, ybuf, gath, brch, back,
    loc_sem, asend, arecv, csend, crecv, dsend, drecv,
):
    T, nr, nch, nco, C, CB, H, W = dims
    quads = nr * nco
    cq = CB // quads
    FH, FW = nr * H, nco * W
    rp = H // nch
    r, ch, co = lax.axis_index("rows"), lax.axis_index("chans"), lax.axis_index("cols")
    q = r * nco + co

    def peer(dr, i, dc):
        return lax.rem(r + dr, nr), lax.rem(ch + i, nch), lax.rem(co + dc, nco)

    def dev(p):
        return {"rows": p[0], "chans": p[1], "cols": p[2]}

    barrier = pltpu.get_barrier_semaphore()

    def greet(i, skip_self):
        for dr in range(nr):
            for dc in range(nco):
                if skip_self and dr == 0 and dc == 0:
                    continue
                pl.semaphore_signal(
                    barrier, inc=1, device_id=dev(peer(dr, i, dc)), device_id_type=MESH
                )

    greet(0, True)

    @pl.loop(1, nch)
    def _(i):
        greet(i, False)

    small = []
    for k, (src, dst) in enumerate(
        ((tapx_hbm, tapx_ref), (tapy_hbm, tapy_ref), (bias_hbm, bias_ref), (weight_hbm, weight_ref))
    ):
        c = pltpu.make_async_copy(src, dst, loc_sem.at[1 + T + k])
        c.start()
        small.append(c)
    own = pltpu.make_async_copy(feat_hbm, feat, loc_sem.at[0])
    mine = []
    for t in range(T):
        c = pltpu.make_async_copy(
            feat_hbm.at[t, pl.ds(pl.multiple_of(q * cq, cq), cq)],
            whole.at[t, r, co],
            loc_sem.at[1 + t],
        )
        c.start()
        mine.append(c)

    pl.semaphore_wait(barrier, nr * nch * nco - 1)

    cs = cq // nch

    def share(t, first, count):
        for dr in range(nr - 1, -1, -1):
            for dc in range(nco):
                if dr == 0 and dc == 0:
                    continue
                p = peer(dr, 0, dc)
                pq = p[0] * nco + p[2]
                pltpu.make_async_remote_copy(
                    src_ref=feat_hbm.at[t, pl.ds(pq * cq + first, count)],
                    dst_ref=whole.at[t, r, co, pl.ds(first, count)],
                    send_sem=asend,
                    recv_sem=arecv.at[t],
                    device_id=dev(p),
                    device_id_type=MESH,
                ).start()

    ahead = 3
    for t in range(min(ahead, T)):
        share(t, 0, cq)

    own.start()

    for c in small:
        c.wait()
    qs = pl.ds(pl.multiple_of(q * cq, cq), cq)
    tx = tapx_ref[qs, :]
    ty = tapy_ref[qs, :]
    tap = iota((KERNEL_TAPS, FW), 0)
    pos = iota((KERNEL_TAPS, FW), 1)
    d = lax.rem(HALF * COLUMN_DILATION - COLUMN_DILATION * tap + FW, FW)
    spread_x = dot(tx, (pos == d).astype(F32).astype(BF16))
    jj = iota((16, FW), 0)
    ww = iota((16, FW), 1)
    reach = HALF * COLUMN_DILATION
    for c in range(cq):
        base = jnp.broadcast_to(spread_x[c : c + 1, :], (16, FW))
        base = pltpu.roll(base, 0, 1, stride=1, stride_axis=0)
        for b in range(FW // 16):
            rolled = base if b == 0 else pltpu.roll(base, 16 * b, 1)
            delta = ww - jj - 16 * b
            keep = (delta <= reach) & (delta >= -reach)
            toep[c, pl.ds(16 * b, 16), :] = jnp.where(keep, rolled, 0.0).astype(BF16)

    KK = cq * FH
    tap = iota((KERNEL_TAPS, FH), 0)
    pos = iota((KERNEL_TAPS, FH), 1)
    own_channel = (iota((cq, KK), 1) // FH) == iota((cq, KK), 0)
    for h in range(FH):
        pick = (pos - h) == ROW_DILATION * (tap - HALF)
        one = dot(ty, pick.astype(F32).astype(BF16))
        tiled = jnp.concatenate([one] * cq, axis=1)
        rowmat[pl.ds(h * cq, cq), :] = jnp.where(own_channel, tiled, 0.0).astype(BF16)

    a = iota((16 * H, 16 * H), 0)
    b = iota((16 * H, 16 * H), 1)
    swap[...] = ((a // H == lax.rem(b, 16)) & (lax.rem(a, H) == b // 16)).astype(F32).astype(BF16)
    diag = jnp.where(
        iota((C, C), 0) == iota((C, C), 1), jnp.broadcast_to(bias_ref[...].astype(F32).reshape(1, C), (C, C)), 0.0
    )
    biasb[...] = dot(diag.astype(BF16), jnp.ones((C, W), BF16))

    for c in mine:
        c.wait()
    own.wait()

    block = ch * quads + q
    chan_rows = pl.ds(pl.multiple_of(block * cq, cq), cq)

    def full_map(t, c):
        bands = [
            jnp.concatenate([whole[t, i, j, c] for j in range(nco)], axis=1) for i in range(nr)
        ]
        return jnp.concatenate(bands, axis=0)

    def conv(t):
        landed = whole.at[0, :, :, pl.ds(0, cq // quads * (quads - 1))]
        pltpu.make_async_copy(landed, landed, arecv.at[t]).wait()

        @pl.loop(0, cq, unroll=4)
        def _(c):
            xbuf[pl.ds(pl.multiple_of(c * FH, FH), FH), :] = dot(full_map(t, c), toep[c]).astype(BF16)

        along = dot(rowmat[...], xbuf[...]).astype(BF16).reshape(FH, cq, FW)
        for k in range(nco):
            ybuf[t, k] = along[:, :, k * W : (k + 1) * W]

        def piece(p):
            return ybuf.at[t, p[2], pl.ds(p[0] * H + p[1] * rp, rp)]

        def push(i, dr, dc):
            p = peer(dr, i, dc)
            pltpu.make_async_remote_copy(
                src_ref=piece(p),
                dst_ref=gath.at[t, :, chan_rows, :],
                send_sem=csend,
                recv_sem=crecv.at[t],
                device_id=dev(p),
                device_id_type=MESH,
            ).start()

        @pl.loop(0, nch - 1)
        def _(s):
            @pl.when(t + ahead < T)
            def _():
                share(t + ahead, s * cs, cs)

            i = lax.rem((nch // 2) * (s + 1) - 1, nch - 1) + 1
            for dr in range(nr):
                for dc in range(nco):
                    push(i, dr, dc)

        @pl.when(t + ahead < T)
        def _():
            share(t + ahead, (nch - 1) * cs, cs)

        for dr in range(nr):
            for dc in range(nco):
                if dr or dc:
                    push(0, dr, dc)
        pltpu.make_async_copy(
            piece((r, ch, co)), gath.at[t, :, chan_rows, :], crecv.at[t]
        ).start()

    def mix(t):
        pltpu.make_async_copy(gath.at[t], gath.at[t], crecv.at[t]).wait()
        for k in range(rp):
            v = dot(weight_ref[...], gath[t, k]) + biasb[...]
            inner = 0.7978845608028654 * (v + 0.044715 * (v * v * v))
            brch[t, k] = (0.5 * v * (1.0 + jnp.tanh(inner))).astype(BF16)

        def piece(pc):
            return brch.at[t, :, pl.ds(pl.multiple_of(pc * CB, CB), CB), :]

        spot = pl.ds(ch * rp, rp)

        @pl.loop(0, nch - 1)
        def _(s):
            i = s + 1
            p = peer(0, i, 0)
            pltpu.make_async_remote_copy(
                src_ref=piece(p[1]),
                dst_ref=back.at[t, spot],
                send_sem=dsend,
                recv_sem=drecv.at[t],
                device_id=dev(p),
                device_id_type=MESH,
            ).start()

        pltpu.make_async_copy(piece(ch), back.at[t, spot], drecv.at[t]).start()

    def finish(t):
        pltpu.make_async_copy(back.at[t], back.at[t], drecv.at[t]).wait()
        for g in range(CB // 16):
            rows = back[t, :, g * 16 : (g + 1) * 16, :].reshape(H * 16, W)
            branch = dot(swap[...], rows).reshape(16, H, W)
            out_ref[t, g * 16 : (g + 1) * 16] = (
                feat[t, g * 16 : (g + 1) * 16].astype(F32) + branch
            ).astype(BF16)

    lag1, lag2 = 3, 5

    @pl.loop(0, T + lag2)
    def _(s):
        @pl.when(s < T)
        def _():
            conv(s)

        @pl.when((s >= lag1) & (s < T + lag1))
        def _():
            mix(s - lag1)

        @pl.when(s >= lag2)
        def _():
            finish(s - lag2)

    sent = whole.at[:, :, :, pl.ds(0, cq // quads * (quads - 1))]
    pltpu.make_async_copy(sent, sent, asend).wait()
    parts = nr * nch * nco
    sent = gath.at[:, :, pl.ds(0, C // parts * (parts - 1)), :]
    pltpu.make_async_copy(sent, sent, csend).wait()
    sent = brch.at[:, :, pl.ds(0, C // nch * (nch - 1)), :]
    pltpu.make_async_copy(sent, sent, dsend).wait()


def per_device(mesh, feature_map, taps_x, taps_y, mix_weight, mix_bias):
    T, CB, H, W = feature_map.shape
    C = mix_weight.shape[0]
    nr, nch, nco = (mesh.shape[a] for a in ("rows", "chans", "cols"))
    quads = nr * nco
    cq = CB // quads
    rp = H // max(nch, 1)
    FH, FW = nr * H, nco * W
    dims = (T, nr, nch, nco, C, CB, H, W)
    return pl.pallas_call(
        functools.partial(section_kernel, dims),
        out_shape=jax.ShapeDtypeStruct(feature_map.shape, BF16),
        in_specs=[pl.BlockSpec(memory_space=pltpu.HBM)] * 5,
        out_specs=pl.BlockSpec(memory_space=pltpu.VMEM),
        scratch_shapes=[
            pltpu.VMEM(taps_x.shape, BF16),
            pltpu.VMEM(taps_y.shape, BF16),
            pltpu.VMEM(mix_weight.shape, BF16),
            pltpu.VMEM((C,), BF16),
            pltpu.VMEM((T, CB, H, W), BF16),
            pltpu.VMEM((T, nr, nco, cq, H, W), BF16),
            pltpu.VMEM((cq, FW, FW), BF16),
            pltpu.VMEM((FH * cq, cq * FH), BF16),
            pltpu.VMEM((16 * H, 16 * H), BF16),
            pltpu.VMEM((C, W), F32),
            pltpu.VMEM((cq * FH, FW), BF16),
            pltpu.VMEM((T, nco, FH, cq, W), BF16),
            pltpu.VMEM((T, rp, C, W), BF16),
            pltpu.VMEM((T, rp, C, W), BF16),
            pltpu.VMEM((T, H, CB, W), BF16),
            pltpu.SemaphoreType.DMA((5 + T,)),
            pltpu.SemaphoreType.DMA,
            pltpu.SemaphoreType.DMA((T,)),
            pltpu.SemaphoreType.DMA,
            pltpu.SemaphoreType.DMA((T,)),
            pltpu.SemaphoreType.DMA,
            pltpu.SemaphoreType.DMA((T,)),
        ],
        compiler_params=pltpu.CompilerParams(
            collective_id=0, has_side_effects=True, vmem_limit_bytes=40 * 1024 * 1024
        ),
    )(*(pltpu.with_memory_space_constraint(v, pltpu.HBM) for v in (feature_map, taps_x, taps_y, mix_weight, mix_bias)))


def fits_kernel(mesh):
    return mesh.shape["rows"] == 2 and mesh.shape["cols"] == 2 and mesh.shape["chans"] == 8


def solution(mesh):
    body = functools.partial(per_device, mesh) if fits_kernel(mesh) else per_device_general
    return jax.shard_map(
        body,
        mesh=mesh,
        in_specs=(
            P("groups", "chans", "rows", "cols"),
            P("chans", None),
            P("chans", None),
            P(),
            P(),
        ),
        out_specs=P("groups", "chans", "rows", "cols"),
        check_vma=False,
    )
```
